256 devices in a mesh: dp: 8 (over x, core), ctx: 8 (over z), mp: 4 (over y).
Axes of the slice: x: 4, y: 4, z: 8, core: 2. Of those that a mesh axis runs over, the one named last changes fastest.
Arguments:
- inputs: bfloat16 [1, 8192, 2048], P(None, ('dp', 'ctx'), 'mp'), may hold values from -6 to 6
- doc_start: int32 [1, 8192], P(None, ('dp', 'ctx')), may hold values 0 or 1
- gate_weight: bfloat16 [256, 8, 512], P(None, 'mp'), may hold values from -0.375 to 0.375
- gate_bias: float32 [8, 512], P('mp'), may hold values from -4 to 4
- decay_rate: float32 [2048], P('mp'), may hold values from 2.4414063e-06 to 0.08, as said below
- cotangent: bfloat16 [1, 8192, 2048], P(None, ('dp', 'ctx'), 'mp'), may hold values from -0.59765625 to 0.59765625
Outputs:
- outputs: bfloat16 [1, 8192, 2048], P(None, ('dp', 'ctx'), 'mp')
- grad_inputs: bfloat16 [1, 8192, 2048], P(None, ('dp', 'ctx'), 'mp')
- grad_gate_weight: float32 [256, 8, 512], P(('dp', 'ctx'), 'mp')
The draws below stay inside these ranges and needn't reach their ends.
Inputs may be any that keep to these rules, and one draw needn't show every extreme that they name: `decay_rate`: each channel's rate is either slow, between 0.02 / 8192 and 0.2 / 8192, or fast, between 0.02 and 0.08, in any mix.
All inputs are finite; a program needn't handle non-finite values. No bound on the sum of `doc_start` on one device may be relied on, other than what follows from the above.
Results may differ from the reference program's by a relative error of at most 0.0028.
Values sent between devices are 32-bit elements; how exact they have to be, the bound alone decides.
No kernel may reach another device: no remote copies, remote signals or barrier semaphores. Data moves between devices by JAX's collectives and lax.ppermute only.
A program may use at most 64 MiB of HBM per device.

```python
import jax
import jax.numpy as jnp
from jax import lax

HEADS = 8
HD = 256
D = 2048
SEQ = 8192
BATCH = 1


def draw_decay_rate(key, part):
    base = jax.random.fold_in(key, 7)
    key_pick, key_slow, key_fast = jax.random.split(base, 3)
    slow_share = 0.5
    picked = jax.random.uniform(key_pick, (D,), jnp.float32)
    slow = jnp.exp(jax.random.uniform(key_slow, (D,), jnp.float32, jnp.log(0.02 / SEQ), jnp.log(0.2 / SEQ)))
    fast = jnp.exp(jax.random.uniform(key_fast, (D,), jnp.float32, jnp.log(0.02), jnp.log(0.08)))
    return jnp.where(picked < slow_share, slow, fast).astype(jnp.float32)


def plant(result, key, low, high):
    place = [jax.random.randint(jax.random.fold_in(key, axis), (), 0, length) for axis, length in enumerate(result.shape)]
    longest = result.shape.index(max(result.shape))
    next_to = place[:longest] + [(place[longest] + 1) % result.shape[longest]] + place[longest + 1:]
    return result.at[tuple(place)].set(low).at[tuple(next_to)].set(high)


def block_scale(key, shape, cuts, smallest, top_value):
    loudness, own = 1.0, jax.random.fold_in(key, 6)
    for dim, blocks in cuts:
        heights = jnp.exp(jax.random.uniform(jax.random.fold_in(own, dim), (blocks,), jnp.float32, smallest / len(cuts), top_value / len(cuts)))
        loudness = loudness * jnp.repeat(heights, shape[dim] // blocks).reshape([-1 if axis == dim else 1 for axis in range(len(shape))])
    return loudness


def gaussian(stream_key, extent, spread, most, cuts=(), dtype=jnp.bfloat16):
    level = block_scale(stream_key, extent, cuts, -0.22, 0.18) if cuts else 1.0
    result = jax.random.normal(stream_key, extent, jnp.float32) * spread * level
    return jnp.minimum(jnp.maximum(result, -most), most).astype(dtype)


def setup_inputs(seed: int = 0) -> dict:
    key_of = jax.random.split(jax.random.key(seed), 7)
    inputs = gaussian(key_of[0], (BATCH, SEQ, D), 1.0, 6.0, ((1, 64), (2, 4)))
    doc_start = plant((jax.random.randint(key_of[1], (BATCH, SEQ), 0, SEQ // 4) < 1).astype(jnp.int32), jax.random.fold_in(key_of[1], 1), 0, 1)
    gate_weight = gaussian(key_of[2], (HD, HEADS, 2 * HD), HD ** -0.5, 0.375, ((1, 4),))
    gate_bias = gaussian(key_of[3], (HEADS, 2 * HD), 1.0, 4.0, ((0, 4),), jnp.float32)
    decay_rate = draw_decay_rate(jax.random.fold_in(key_of[6], 71), 0)
    cotangent = gaussian(key_of[5], (BATCH, SEQ, D), 0.1, 0.59765625, ((1, 64), (2, 4)))
    return {"inputs": inputs, "doc_start": doc_start, "gate_weight": gate_weight, "gate_bias": gate_bias, "decay_rate": decay_rate, "cotangent": cotangent}


def linear_link(first, second):
    return (first[0] * second[0], second[0] * first[1] + second[1])

def head_pass(pieces):
    x_head, w_head, b_head, r_head, g_head, keep = pieces
    width = x_head.shape[2]
    x_float = x_head.astype(jnp.float32)
    pre = jnp.einsum('bsk,km->bsm', x_float, w_head.astype(jnp.float32)) + b_head
    rgate = jax.nn.sigmoid(pre[..., :width])
    igate = jax.nn.sigmoid(pre[..., width:])
    decay = jnp.exp(-8.0 * rgate * r_head)
    keep3 = keep[..., None]
    carry = decay * keep3
    root = jnp.sqrt(1.0 - decay * decay + 0.01)
    scale = jnp.where(keep3 > 0.5, root, jnp.float32(1.0))
    drive = scale * igate * x_float
    cumul, state = lax.associative_scan(linear_link, (carry, drive), axis=1)
    outputs = state.astype(jnp.bfloat16)
    grad_out = g_head.astype(jnp.float32)
    ones_col = jnp.ones_like(carry[:, :1])
    shifted = jnp.concatenate([carry[:, 1:], ones_col], axis=1)
    pcum, adjoint = lax.associative_scan(linear_link, (shifted, grad_out), reverse=True, axis=1)
    previous = jnp.concatenate([jnp.zeros_like(state[:, :1]), state[:, :-1]], axis=1)
    dscale = jnp.where(keep3 > 0.5, -decay * decay / root, jnp.float32(0.0))
    dlog = adjoint * keep3 * decay * previous + adjoint * igate * x_float * dscale
    dgate = dlog * (-8.0 * r_head) * rgate * (1.0 - rgate)
    dinput = adjoint * scale * x_float * igate * (1.0 - igate)
    dpre = jnp.concatenate([dgate, dinput], axis=-1).astype(jnp.bfloat16)
    dpre_float = dpre.astype(jnp.float32)
    grad_x = adjoint * scale * igate + jnp.einsum('bsm,km->bsk', dpre_float, w_head.astype(jnp.float32))
    grad_w = jnp.einsum('bsk,bsm->km', x_float, dpre_float)
    return (outputs, grad_x.astype(jnp.bfloat16), grad_w)

def reference(inputs, doc_start, gate_weight, gate_bias, decay_rate, cotangent):
    batch_rows, seq_len, width_all = inputs.shape
    heads = gate_weight.shape[1]
    head_dim = gate_weight.shape[0]
    keep = 1.0 - doc_start.astype(jnp.float32)
    x_heads = jnp.moveaxis(inputs.reshape(batch_rows, seq_len, heads, head_dim), 2, 0)
    g_heads = jnp.moveaxis(cotangent.reshape(batch_rows, seq_len, heads, head_dim), 2, 0)
    w_heads = jnp.moveaxis(gate_weight, 1, 0)
    r_heads = decay_rate.reshape(heads, head_dim)

    def one_head(items):
        x_head, w_head, b_head, r_head, g_head = items
        return head_pass((x_head, w_head, b_head, r_head, g_head, keep))
    outs, grads, wgrads = lax.map(one_head, (x_heads, w_heads, gate_bias, r_heads, g_heads))
    outputs = jnp.moveaxis(outs, 0, 2).reshape(batch_rows, seq_len, width_all)
    grad_inputs = jnp.moveaxis(grads, 0, 2).reshape(batch_rows, seq_len, width_all)
    grad_gate_weight = jnp.moveaxis(wgrads, 0, 1)
    return (outputs, grad_inputs, grad_gate_weight)
```

```python
import jax
import jax.numpy as jnp
from jax import lax
from jax.experimental import pallas as pl
from jax.experimental.pallas import tpu as pltpu
from jax.sharding import Mesh, PartitionSpec as P

LANES = 128
SUB = 8


def column_scan(decays, drives, backward):
    rows = decays.shape[0]
    groups = rows // SUB
    a = decays.reshape(groups, SUB, LANES)
    b = drives.reshape(groups, SUB, LANES)
    place = lax.broadcasted_iota(jnp.int32, (groups, SUB, LANES), 1)
    step = 1
    while step < SUB:
        if backward:
            shift, ok = SUB - step, place < SUB - step
        else:
            shift, ok = step, place >= step
        a_far = jnp.where(ok, pltpu.roll(a, shift, 1), 1.0)
        b_far = jnp.where(ok, pltpu.roll(b, shift, 1), 0.0)
        b = a * b_far + b
        a = a * a_far
        step *= 2
    order = range(groups - 1, -1, -1) if backward else range(groups)
    edge = 0 if backward else SUB - 1
    a_in = jnp.ones((1, LANES), jnp.float32)
    b_in = jnp.zeros((1, LANES), jnp.float32)
    a_out, b_out = [None] * groups, [None] * groups
    for g in order:
        a_out[g] = a[g] * a_in
        b_out[g] = a[g] * b_in + b[g]
        a_in = a_out[g][edge : edge + 1]
        b_in = b_out[g][edge : edge + 1]
    return jnp.concatenate(a_out, 0), jnp.concatenate(b_out, 0), a_in, b_in


def local_kernel(
    x_ref, doc_ref, w_ref, bias_ref, rate_ref, cot_ref,
    summary_ref, k1_ref, k2_ref, k3_ref, k4_ref, cum_ref, ls_ref, pc_ref, la_ref,
):
    rows, width = x_ref.shape
    heads, head_dim, _ = w_ref.shape
    doc = jnp.broadcast_to(doc_ref[...].astype(jnp.float32), (LANES, rows))
    keep = 1.0 - jnp.transpose(doc)
    row = lax.broadcasted_iota(jnp.int32, (rows, LANES), 0)
    for h in range(heads):
        pre = jnp.dot(
            x_ref[:, h * head_dim : (h + 1) * head_dim], w_ref[h], preferred_element_type=jnp.float32
        ) + bias_ref[h : h + 1, :]
        for part in range(head_dim // LANES):
            q = h * (head_dim // LANES) + part
            lanes = slice(q * LANES, (q + 1) * LANES)
            rgate = jax.nn.sigmoid(pre[:, part * LANES : (part + 1) * LANES])
            igate = jax.nn.sigmoid(pre[:, head_dim + part * LANES : head_dim + (part + 1) * LANES])
            x = x_ref[:, lanes].astype(jnp.float32)
            rate8 = -8.0 * rate_ref[:, lanes]
            decay = jnp.exp(rate8 * rgate)
            carry = decay * keep
            square = decay * decay
            root = jnp.sqrt(1.0 - square + 0.01)
            kept = keep > 0.5
            scale = jnp.where(kept, root, 1.0)
            dscale = jnp.where(kept, -square / root, 0.0)
            slope = rate8 * (rgate * (1.0 - rgate))
            k4 = scale * igate
            drive = k4 * x
            k1_ref[:, lanes] = carry * slope
            k2_ref[:, lanes] = igate * x * dscale * slope
            k3_ref[:, lanes] = drive * (1.0 - igate)
            k4_ref[:, lanes] = k4
            cum, state, product, last = column_scan(carry, drive, False)
            cum_ref[:, lanes] = cum
            ls_ref[:, lanes] = state
            cot = cot_ref[:, lanes].astype(jnp.float32)
            ahead = jnp.where(row == rows - 1, 1.0, pltpu.roll(carry, rows - 1, 0))
            pc, adjoint, _, first = column_scan(ahead, cot, True)
            pc_ref[:, lanes] = pc
            la_ref[:, lanes] = adjoint
            summary_ref[0, q : q + 1, :] = product
            summary_ref[1, q : q + 1, :] = last
            summary_ref[2, q : q + 1, :] = carry[0:1] * first


def finish_kernel(
    place_ref, all_ref, x_ref, w_ref, k1_ref, k2_ref, k3_ref, k4_ref, cum_ref, ls_ref, pc_ref, la_ref,
    out_ref, gx_ref, mine_ref, other_ref, gw_ref,
):
    rows, width = x_ref.shape
    heads, head_dim, _ = w_ref.shape
    mine, core = place_ref[0], place_ref[1]
    count = all_ref.shape[0]
    entering = jnp.zeros(all_ref.shape[2:], jnp.float32)
    arriving = entering
    for j in range(count - 1):
        entering = jnp.where(j < mine, all_ref[j, 0] * entering + all_ref[j, 1], entering)
        i = count - 1 - j
        arriving = jnp.where(i > mine, all_ref[i, 0] * arriving + all_ref[i, 2], arriving)
    row = lax.broadcasted_iota(jnp.int32, (rows, LANES), 0)
    parts = head_dim // LANES
    for h in range(heads):
        gate, drive, direct = [], [], []
        for part in range(parts):
            q = h * parts + part
            lanes = slice(q * LANES, (q + 1) * LANES)
            before = entering[q : q + 1]
            state = ls_ref[:, lanes] + cum_ref[:, lanes] * before
            out_ref[:, lanes] = state.astype(jnp.bfloat16)
            previous = jnp.where(row == 0, before, pltpu.roll(state, 1, 0))
            adjoint = la_ref[:, lanes] + pc_ref[:, lanes] * arriving[q : q + 1]
            gate.append((adjoint * (k1_ref[:, lanes] * previous + k2_ref[:, lanes])).astype(jnp.bfloat16))
            drive.append((adjoint * k3_ref[:, lanes]).astype(jnp.bfloat16))
            direct.append(adjoint * k4_ref[:, lanes])
        dpre = jnp.concatenate(gate + drive, axis=1)
        back = lax.dot_general(dpre, w_ref[h], (((1,), (1,)), ((), ())), preferred_element_type=jnp.float32)
        columns = slice(h * head_dim, (h + 1) * head_dim)
        gx_ref[:, columns] = (jnp.concatenate(direct, axis=1) + back).astype(jnp.bfloat16)
        gw_ref[:, h * 2 * head_dim : (h + 1) * 2 * head_dim] = lax.dot_general(
            x_ref[:, columns], dpre, (((0,), (0,)), ((), ())), preferred_element_type=jnp.float32
        )
    chunks, depth = mine_ref.shape[0], mine_ref.shape[1]
    for c in range(chunks):
        start = pl.multiple_of(c * 2 * depth + core * depth, depth)
        mine_ref[c] = gw_ref[pl.ds(start, depth), :]
        start = pl.multiple_of(c * 2 * depth + (1 - core) * depth, depth)
        other_ref[c] = gw_ref[pl.ds(start, depth), :]


def per_device(inputs, doc_start, gate_weight, gate_bias, decay_rate, cotangent):
    _, rows, width = inputs.shape
    head_dim, heads, wide = gate_weight.shape
    n_x, n_core, n_z = lax.axis_size("x"), lax.axis_size("core"), lax.axis_size("z")
    blocks = n_x * n_core * n_z
    x = inputs.reshape(rows, width)
    weight = jnp.moveaxis(gate_weight, 1, 0)
    f32 = jnp.float32
    field = jax.ShapeDtypeStruct((rows, width), f32)
    params = pltpu.CompilerParams(vmem_limit_bytes=24 << 20)
    tiles = width // LANES
    summary, *saved = pl.pallas_call(
        local_kernel,
        out_shape=[jax.ShapeDtypeStruct((3, tiles, LANES), f32)] + [field] * 8,
        compiler_params=params,
        name="local_scans",
    )(x, doc_start, weight, gate_bias, decay_rate.reshape(1, width), cotangent.reshape(rows, width))
    spread = jnp.broadcast_to(summary, (blocks,) + summary.shape)
    everyone = lax.all_to_all(spread, ("x", "core", "z"), 0, 0)
    core = lax.axis_index("core")
    place = jnp.stack([(lax.axis_index("x") * n_core + core) * n_z + lax.axis_index("z"), core])
    vmem = pl.BlockSpec(memory_space=pltpu.VMEM)
    depth = head_dim // (n_x * n_core)
    half = jax.ShapeDtypeStruct((n_x, depth, heads * wide), f32)
    outputs, grad_inputs, mine, other = pl.pallas_call(
        finish_kernel,
        out_shape=[
            jax.ShapeDtypeStruct((rows, width), jnp.bfloat16),
            jax.ShapeDtypeStruct((rows, width), jnp.bfloat16),
            half,
            half,
        ],
        in_specs=[pl.BlockSpec(memory_space=pltpu.SMEM)] + [vmem] * 11,
        scratch_shapes=[pltpu.VMEM((head_dim, heads * wide), f32)],
        compiler_params=params,
        name="finish",
    )(place, everyone, x, weight, *saved)
    swapped = lax.ppermute(other, "core", [(0, 1), (1, 0)])
    pair = (mine + swapped).reshape(n_x * n_z, depth // n_z, heads * wide)
    pieces = lax.all_to_all(pair, ("x", "z"), 0, 0)
    grad_gate_weight = pieces.sum(0).reshape(depth // n_z, heads, wide)
    return (outputs[None], grad_inputs[None], grad_gate_weight)


def solution(mesh):
    n_dp, n_ctx, n_mp = mesh.devices.shape
    fine = Mesh(mesh.devices.reshape(n_dp // 2, 2, n_ctx, n_mp), ("x", "core", "z", "mp"))
    place = ("x", "core", "z")
    return jax.shard_map(
        per_device,
        mesh=fine,
        in_specs=(P(None, place, "mp"), P(None, place), P(None, "mp", None), P("mp", None), P("mp"), P(None, place, "mp")),
        out_specs=(P(None, place, "mp"), P(None, place, "mp"), P(place, "mp", None)),
        check_vma=False,
    )
```

```python
import jax
import jax.numpy as jnp
from jax import lax
from jax.experimental import pallas as pl
from jax.experimental.pallas import tpu as pltpu
from jax.sharding import Mesh, PartitionSpec as P

LANES = 128
SUB = 8
F32 = jnp.float32
BF16 = jnp.bfloat16


def column_scan(decays, drives, backward):
    rows = decays.shape[0]
    groups = rows // SUB
    a = decays.reshape(groups, SUB, LANES)
    b = drives.reshape(groups, SUB, LANES)
    place = lax.broadcasted_iota(jnp.int32, (groups, SUB, LANES), 1)
    step = 1
    while step < SUB:
        if backward:
            shift, ok = SUB - step, place < SUB - step
        else:
            shift, ok = step, place >= step
        a_far = jnp.where(ok, pltpu.roll(a, shift, 1), 1.0)
        b_far = jnp.where(ok, pltpu.roll(b, shift, 1), 0.0)
        b = a * b_far + b
        a = a * a_far
        step *= 2
    order = range(groups - 1, -1, -1) if backward else range(groups)
    edge = 0 if backward else SUB - 1
    a_in = jnp.ones((1, LANES), F32)
    b_in = jnp.zeros((1, LANES), F32)
    a_out, b_out = [None] * groups, [None] * groups
    for g in order:
        a_out[g] = a[g] * a_in
        b_out[g] = a[g] * b_in + b[g]
        a_in = a_out[g][edge : edge + 1]
        b_in = b_out[g][edge : edge + 1]
    return jnp.concatenate(a_out, 0), jnp.concatenate(b_out, 0), a_in, b_in


def pack_kernel(x_ref, cot_ref, doc_ref, _, send_ref, own_ref):
    rows, width = x_ref.shape
    half = width // 2
    first = lax.axis_index("core") == 0
    for r, ref in enumerate((x_ref, cot_ref)):
        both = ref[...].astype(F32)
        send_ref[r * rows : (r + 1) * rows, :] = jnp.where(first, both[:, half:], both[:, :half])
        own_ref[r * rows : (r + 1) * rows, :] = jnp.where(first, both[:, :half], both[:, half:])
    doc = jnp.broadcast_to(doc_ref[...].astype(F32), (SUB, rows))
    doc = jnp.concatenate([doc] * (half // rows), axis=1)
    send_ref[2 * rows : 2 * rows + SUB, :] = doc
    own_ref[2 * rows : 2 * rows + SUB, :] = doc


def local_scans(pack_ref, w_ref, bias_ref, rate_ref, x_ref, k1_ref, k2_ref, k3_ref, k4_ref, cum_ref, ls_ref, pc_ref, la_ref):
    rows, half = x_ref.shape
    core = lax.axis_index("core")
    row = lax.broadcasted_iota(jnp.int32, (rows, LANES), 0)
    x_ref[...] = pack_ref[:rows].astype(BF16)
    rate8 = -8.0 * jnp.where(core == 0, rate_ref[:, :half], rate_ref[:, half:])
    pre = jnp.dot(x_ref[...], w_ref[core], preferred_element_type=F32) + bias_ref[pl.ds(core, 1), :]
    keep = 1.0 - jnp.transpose(jnp.broadcast_to(pack_ref[2 * rows : 2 * rows + 1, :rows], (LANES, rows)))
    kept = keep > 0.5
    ends = []
    for part in range(half // LANES):
        lanes = slice(part * LANES, (part + 1) * LANES)
        rgate = jax.nn.sigmoid(pre[:, lanes])
        igate = jax.nn.sigmoid(pre[:, half + part * LANES : half + (part + 1) * LANES])
        x = pack_ref[:rows, lanes]
        rate = rate8[:, lanes]
        decay = jnp.exp(rate * rgate)
        carry = decay * keep
        square = decay * decay
        root = jnp.sqrt(1.0 - square + 0.01)
        scale = jnp.where(kept, root, 1.0)
        dscale = jnp.where(kept, -square / root, 0.0)
        slope = rate * (rgate * (1.0 - rgate))
        k4 = scale * igate
        drive = k4 * x
        k1_ref[:, lanes] = carry * slope
        k2_ref[:, lanes] = igate * x * dscale * slope
        k3_ref[:, lanes] = drive * (1.0 - igate)
        k4_ref[:, lanes] = k4
        cum, state, product, last = column_scan(carry, drive, False)
        cum_ref[:, lanes] = cum
        ls_ref[:, lanes] = state
        ahead = jnp.where(row == rows - 1, 1.0, pltpu.roll(carry, rows - 1, 0))
        pc, adjoint, _, top = column_scan(ahead, pack_ref[rows : 2 * rows, lanes], True)
        pc_ref[:, lanes] = pc
        la_ref[:, lanes] = adjoint
        ends.append((product, last, carry[0:1] * top))
    return ends


def own_kernel(pack_ref, w_ref, bias_ref, rate_ref, summary_ref, *refs):
    for part, values in enumerate(local_scans(pack_ref, w_ref, bias_ref, rate_ref, *refs)):
        for i, value in enumerate(values):
            summary_ref[i, part : part + 1, :] = value


def got_kernel(pack_ref, w_ref, bias_ref, rate_ref, own_ref, spread_ref, *refs):
    *refs, summary_ref = refs
    core = lax.axis_index("core")
    ends = local_scans(pack_ref, w_ref, bias_ref, rate_ref, *refs)
    for part, values in enumerate(ends):
        for i, value in enumerate(values):
            summary_ref[i, pl.ds(core * len(ends) + part, 1), :] = own_ref[i, part : part + 1, :]
            summary_ref[i, pl.ds((1 - core) * len(ends) + part, 1), :] = value
    summary = summary_ref[...]
    for j in range(spread_ref.shape[0]):
        spread_ref[j] = summary


def fold(all_ref, order, kind, base, wanted=None):
    product = jnp.ones(all_ref.shape[2:], F32)
    value = jnp.zeros(all_ref.shape[2:], F32)
    for z in order:
        a, b = all_ref[base + z, 0], all_ref[base + z, kind]
        if wanted is not None:
            a, b = jnp.where(wanted(z), a, 1.0), jnp.where(wanted(z), b, 0.0)
        value = a * value + b
        product = product * a
    return product, value


def edges(all_ref, kind, x, z, n_x, n_z, backward):
    half = all_ref.shape[2] // 2
    cores = (slice(0, half), slice(half, 2 * half))
    near, far = (cores[1], cores[0]) if backward else cores
    order = range(n_z - 1, -1, -1) if backward else range(n_z)
    apply = lambda link, at, value: link[0][at] * value + link[1][at]
    carried = jnp.zeros((half, LANES), F32)
    for i in range(n_x - 1, 0, -1) if backward else range(n_x - 1):
        link = fold(all_ref, order, kind, i * n_z)
        carried = jnp.where(i > x if backward else i < x, apply(link, far, apply(link, near, carried)), carried)
    base = x * n_z
    whole = fold(all_ref, order, kind, base)
    partial = fold(all_ref, order, kind, base, (lambda i: i > z) if backward else (lambda i: i < z))
    ahead = apply(partial, near, carried)
    behind = apply(partial, far, apply(whole, near, carried))
    return (behind, ahead) if backward else (ahead, behind)


def finish_kernel(n_x, n_z, all_ref, *refs):
    own, got, (out_ref, send_ref, dpre_ref, direct_ref, gw_ref) = refs[:9], refs[9:18], refs[18:]
    rows, half = out_ref.shape
    first = lax.axis_index("core") == 0
    at_x, at_z = lax.axis_index("x"), lax.axis_index("z")
    entering = edges(all_ref, 1, at_x, at_z, n_x, n_z, False)
    arriving = edges(all_ref, 2, at_x, at_z, n_x, n_z, True)
    row = lax.broadcasted_iota(jnp.int32, (rows, LANES), 0)
    weight_grad = 0.0
    for block, (x_ref, k1_ref, k2_ref, k3_ref, k4_ref, cum_ref, ls_ref, pc_ref, la_ref) in enumerate((own, got)):
        there = slice(block * rows, (block + 1) * rows)
        before = jnp.where(first, entering[block], entering[1 - block])
        after = jnp.where(first, arriving[block], arriving[1 - block])
        for part in range(half // LANES):
            lanes = slice(part * LANES, (part + 1) * LANES)
            start = before[part : part + 1]
            state = ls_ref[:, lanes] + cum_ref[:, lanes] * start
            if block == 0:
                out_ref[:, lanes] = state.astype(BF16)
            else:
                send_ref[:, lanes] = state
            previous = jnp.where(row == 0, start, pltpu.roll(state, 1, 0))
            adjoint = la_ref[:, lanes] + pc_ref[:, lanes] * after[part : part + 1]
            dpre_ref[there, lanes] = (adjoint * (k1_ref[:, lanes] * previous + k2_ref[:, lanes])).astype(BF16)
            far = slice(half + part * LANES, half + (part + 1) * LANES)
            dpre_ref[there, far] = (adjoint * k3_ref[:, lanes]).astype(BF16)
            direct_ref[there, lanes] = adjoint * k4_ref[:, lanes]
        weight_grad = weight_grad + lax.dot_general(
            x_ref[...], dpre_ref[there, :], (((0,), (0,)), ((), ())), preferred_element_type=F32
        )
    depth = SUB // 2
    low = lax.broadcasted_iota(jnp.int32, (SUB, 2 * half), 0) < depth
    for i in range(n_x):
        for pair in range(n_z // 2):
            u = weight_grad[i * 2 * n_z * depth + pair * SUB :][:SUB]
            v = weight_grad[(i * 2 + 1) * n_z * depth + pair * SUB :][:SUB]
            gw_ref[i * n_z + 2 * pair] = jnp.where(low, u, pltpu.roll(v, depth, 0))
            gw_ref[i * n_z + 2 * pair + 1] = jnp.where(low, pltpu.roll(u, depth, 0), v)


def inputs_kernel(dpre_ref, direct_ref, w_ref, states_ref, gx_ref, send_ref):
    rows = gx_ref.shape[0]
    core = lax.axis_index("core")
    back = lax.dot_general(dpre_ref[...], w_ref[core], (((1,), (1,)), ((), ())), preferred_element_type=F32)
    total = direct_ref[...] + back
    gx_ref[...] = total[:rows].astype(BF16)
    send_ref[:rows] = states_ref[...]
    send_ref[rows:] = total[rows:]


def unswap_kernel(out_ref, gx_ref, got_ref, outputs_ref, grad_ref, order_ref):
    rows, half = out_ref.shape
    first = lax.axis_index("core") == 0
    for r, (own, whole) in enumerate(((out_ref, outputs_ref), (gx_ref, grad_ref))):
        mine = own[...].astype(F32)
        got = got_ref[r * rows : (r + 1) * rows]
        whole[:, :half] = jnp.where(first, mine, got).astype(BF16)
        whole[:, half:] = jnp.where(first, got, mine).astype(BF16)
    order_ref[...] = jnp.zeros_like(order_ref)


def sum_kernel(pieces_ref, _, keep_ref, send_ref):
    total = pieces_ref[0]
    for j in range(1, pieces_ref.shape[0]):
        total = total + pieces_ref[j]
    first = lax.axis_index("core") == 0
    depth = SUB // 2
    keep_ref[...] = jnp.where(first, total[:depth], total[depth:])
    send_ref[...] = jnp.where(first, total[depth:], total[:depth])


def join_kernel(keep_ref, got_ref, grad_ref):
    first = lax.axis_index("core") == 0
    keep, got = keep_ref[...], got_ref[...]
    grad_ref[:, 0, :] = jnp.where(first, keep, got)
    grad_ref[:, 1, :] = jnp.where(first, got, keep)


def per_device(inputs, doc_start, gate_weight, gate_bias, decay_rate, cotangent):
    _, rows, width = inputs.shape
    head_dim, heads, wide = gate_weight.shape
    n_x, n_z = lax.axis_size("x"), lax.axis_size("z")
    chips = n_x * n_z
    half = width // 2
    depth = SUB // 2
    shape = jax.ShapeDtypeStruct
    vmem = pl.BlockSpec(memory_space=pltpu.VMEM)

    def call(kernel, operands, outs, name, scratch=()):
        return pl.pallas_call(
            kernel,
            out_shape=outs,
            in_specs=[vmem] * len(operands),
            scratch_shapes=scratch,
            compiler_params=pltpu.CompilerParams(vmem_limit_bytes=16 << 20),
            name=name,
        )(*operands)

    swap = lambda value: lax.ppermute(value, "core", [(0, 1), (1, 0)])
    packed = shape((2 * rows + SUB, half), F32)
    gates = (jnp.moveaxis(gate_weight, 1, 0), gate_bias, decay_rate.reshape(1, width))
    operands = (inputs.reshape(rows, width), cotangent.reshape(rows, width), doc_start, gates[0])
    send, own = call(pack_kernel, operands, [packed] * 2, "pack")
    got = swap(send)
    fields = [shape((rows, half), BF16)] + [shape((rows, half), F32)] * 8
    tiles = half // LANES
    summary, *own = call(own_kernel, (own, *gates), [shape((3, tiles, LANES), F32)] + fields, "own_scans")
    spread, *got = call(
        got_kernel,
        (got, *gates, summary),
        [shape((chips, 3, 2 * tiles, LANES), F32)] + fields,
        "got_scans",
        [pltpu.VMEM((3, 2 * tiles, LANES), F32)],
    )
    everyone = lax.all_to_all(spread, ("x", "z"), 0, 0)
    out, states, dpre, direct, gw = call(
        lambda *refs: finish_kernel(n_x, n_z, *refs),
        (everyone, *own, *got),
        [
            shape((rows, half), BF16),
            shape((rows, half), F32),
            shape((2 * rows, wide), BF16),
            shape((2 * rows, half), F32),
            shape((chips, SUB, wide), F32),
        ],
        "finish",
    )
    pieces = lax.all_to_all(gw, ("x", "z"), 0, 0)
    gx, send = call(
        inputs_kernel, (dpre, direct, gates[0], states), [shape((rows, half), BF16), shape((2 * rows, half), F32)], "grad_inputs"
    )
    outputs, grad_inputs, order = call(
        unswap_kernel, (out, gx, swap(send)), [shape((rows, width), BF16)] * 2 + [shape((SUB, LANES), F32)], "unswap"
    )
    keep, give = call(sum_kernel, (pieces, order), [shape((depth, wide), F32)] * 2, "sum")
    grad_gate_weight = call(join_kernel, (keep, swap(give)), shape((depth, heads, wide), F32), "join")
    return (outputs[None], grad_inputs[None], grad_gate_weight)


def solution(mesh):
    n_dp, n_ctx, n_mp = mesh.devices.shape
    fine = Mesh(mesh.devices.reshape(n_dp // 2, 2, n_ctx, n_mp), ("x", "core", "z", "mp"))
    place = ("x", "core", "z")
    return jax.shard_map(
        per_device,
        mesh=fine,
        in_specs=(P(None, place, "mp"), P(None, place), P(None, "mp", None), P("mp", None), P("mp"), P(None, place, "mp")),
        out_specs=(P(None, place, "mp"), P(None, place, "mp"), P(place, "mp", None)),
        check_vma=False,
    )
```

```python
import jax
import jax.numpy as jnp
from jax import lax
from jax.experimental import pallas as pl
from jax.experimental.pallas import tpu as pltpu
from jax.sharding import Mesh, PartitionSpec as P

LANES = 128
SUB = 8
F32 = jnp.float32
BF16 = jnp.bfloat16


def column_scan(decays, drives, backward):
    rows = decays.shape[0]
    groups = rows // SUB
    a = decays.reshape(groups, SUB, LANES)
    b = drives.reshape(groups, SUB, LANES)
    place = lax.broadcasted_iota(jnp.int32, (groups, SUB, LANES), 1)
    step = 1
    while step < SUB:
        if backward:
            shift, ok = SUB - step, place < SUB - step
        else:
            shift, ok = step, place >= step
        a_far = jnp.where(ok, pltpu.roll(a, shift, 1), 1.0)
        b_far = jnp.where(ok, pltpu.roll(b, shift, 1), 0.0)
        b = a * b_far + b
        a = a * a_far
        step *= 2
    order = range(groups - 1, -1, -1) if backward else range(groups)
    edge = 0 if backward else SUB - 1
    a_in = jnp.ones((1, LANES), F32)
    b_in = jnp.zeros((1, LANES), F32)
    a_out, b_out = [None] * groups, [None] * groups
    for g in order:
        a_out[g] = a[g] * a_in
        b_out[g] = a[g] * b_in + b[g]
        a_in = a_out[g][edge : edge + 1]
        b_in = b_out[g][edge : edge + 1]
    return jnp.concatenate(a_out, 0), jnp.concatenate(b_out, 0), a_in, b_in


def head_kernel(order_ref):
    order_ref[...] = jnp.zeros_like(order_ref)


def pack_kernel(x_ref, cot_ref, doc_ref, bias_ref, rate_ref, order_ref, send_ref, own_ref):
    rows, width = x_ref.shape
    half = width // 2
    first = lax.axis_index("core") == 0
    for r, ref in enumerate((x_ref, cot_ref)):
        both = ref[...].astype(F32)
        send_ref[r * rows : (r + 1) * rows, :] = jnp.where(first, both[:, half:], both[:, :half])
        own_ref[r * rows : (r + 1) * rows, :] = jnp.where(first, both[:, :half], both[:, half:])
    doc = jnp.broadcast_to(doc_ref[...].astype(F32), (SUB, rows))
    doc = jnp.concatenate([doc] * (half // rows), axis=1)
    send_ref[2 * rows : 2 * rows + SUB, :] = doc
    own_ref[2 * rows : 2 * rows + SUB, :] = doc


def local_scans(pack_ref, w_ref, bias_ref, rate_ref, x_ref, k1_ref, k2_ref, k3_ref, k4_ref, cum_ref, ls_ref, pc_ref, la_ref):
    rows, half = x_ref.shape
    core = lax.axis_index("core")
    row = lax.broadcasted_iota(jnp.int32, (rows, LANES), 0)
    x_ref[...] = pack_ref[:rows].astype(BF16)
    rate8 = -8.0 * jnp.where(core == 0, rate_ref[:, :half], rate_ref[:, half:])
    pre = jnp.dot(x_ref[...], w_ref[core], preferred_element_type=F32) + bias_ref[pl.ds(core, 1), :]
    keep = 1.0 - jnp.transpose(jnp.broadcast_to(pack_ref[2 * rows : 2 * rows + 1, :rows], (LANES, rows)))
    kept = keep > 0.5
    ends = []
    for part in range(half // LANES):
        lanes = slice(part * LANES, (part + 1) * LANES)
        rgate = jax.nn.sigmoid(pre[:, lanes])
        igate = jax.nn.sigmoid(pre[:, half + part * LANES : half + (part + 1) * LANES])
        x = pack_ref[:rows, lanes]
        rate = rate8[:, lanes]
        decay = jnp.exp(rate * rgate)
        carry = decay * keep
        square = decay * decay
        root = jnp.sqrt(1.0 - square + 0.01)
        scale = jnp.where(kept, root, 1.0)
        dscale = jnp.where(kept, -square / root, 0.0)
        slope = rate * (rgate * (1.0 - rgate))
        k4 = scale * igate
        drive = k4 * x
        k1_ref[:, lanes] = carry * slope
        k2_ref[:, lanes] = igate * x * dscale * slope
        k3_ref[:, lanes] = drive * (1.0 - igate)
        k4_ref[:, lanes] = k4
        cum, state, product, last = column_scan(carry, drive, False)
        cum_ref[:, lanes] = cum
        ls_ref[:, lanes] = state
        ahead = jnp.where(row == rows - 1, 1.0, pltpu.roll(carry, rows - 1, 0))
        pc, adjoint, _, top = column_scan(ahead, pack_ref[rows : 2 * rows, lanes], True)
        pc_ref[:, lanes] = pc
        la_ref[:, lanes] = adjoint
        ends.append((product, last, carry[0:1] * top))
    return ends


def own_kernel(pack_ref, w_ref, bias_ref, rate_ref, summary_ref, *refs):
    for part, values in enumerate(local_scans(pack_ref, w_ref, bias_ref, rate_ref, *refs)):
        for i, value in enumerate(values):
            summary_ref[i, part : part + 1, :] = value


def got_kernel(pack_ref, w_ref, bias_ref, rate_ref, own_ref, summary_ref, *refs):
    core = lax.axis_index("core")
    ends = local_scans(pack_ref, w_ref, bias_ref, rate_ref, *refs)
    for part, values in enumerate(ends):
        for i, value in enumerate(values):
            summary_ref[i, pl.ds(core * len(ends) + part, 1), :] = own_ref[i, part : part + 1, :]
            summary_ref[i, pl.ds((1 - core) * len(ends) + part, 1), :] = value


def spread_kernel(summary_ref, _, spread_ref):
    summary = summary_ref[...]
    for j in range(spread_ref.shape[0]):
        spread_ref[j] = summary


def fold(all_ref, order, kind, base, wanted=None):
    product = jnp.ones(all_ref.shape[2:], F32)
    value = jnp.zeros(all_ref.shape[2:], F32)
    for z in order:
        a, b = all_ref[base + z, 0], all_ref[base + z, kind]
        if wanted is not None:
            a, b = jnp.where(wanted(z), a, 1.0), jnp.where(wanted(z), b, 0.0)
        value = a * value + b
        product = product * a
    return product, value


def edges(all_ref, kind, x, z, n_x, n_z, backward):
    half = all_ref.shape[2] // 2
    cores = (slice(0, half), slice(half, 2 * half))
    near, far = (cores[1], cores[0]) if backward else cores
    order = range(n_z - 1, -1, -1) if backward else range(n_z)
    apply = lambda link, at, value: link[0][at] * value + link[1][at]
    carried = jnp.zeros((half, LANES), F32)
    for i in range(n_x - 1, 0, -1) if backward else range(n_x - 1):
        link = fold(all_ref, order, kind, i * n_z)
        carried = jnp.where(i > x if backward else i < x, apply(link, far, apply(link, near, carried)), carried)
    base = x * n_z
    whole = fold(all_ref, order, kind, base)
    partial = fold(all_ref, order, kind, base, (lambda i: i > z) if backward else (lambda i: i < z))
    ahead = apply(partial, near, carried)
    behind = apply(partial, far, apply(whole, near, carried))
    return (behind, ahead) if backward else (ahead, behind)


def finish_kernel(n_x, n_z, all_ref, *refs):
    own, got, (out_ref, send_ref, dpre_ref, direct_ref, gw_ref) = refs[:9], refs[9:18], refs[18:]
    rows, half = out_ref.shape
    first = lax.axis_index("core") == 0
    at_x, at_z = lax.axis_index("x"), lax.axis_index("z")
    entering = edges(all_ref, 1, at_x, at_z, n_x, n_z, False)
    arriving = edges(all_ref, 2, at_x, at_z, n_x, n_z, True)
    row = lax.broadcasted_iota(jnp.int32, (rows, LANES), 0)
    weight_grad = 0.0
    for block, (x_ref, k1_ref, k2_ref, k3_ref, k4_ref, cum_ref, ls_ref, pc_ref, la_ref) in enumerate((own, got)):
        there = slice(block * rows, (block + 1) * rows)
        before = jnp.where(first, entering[block], entering[1 - block])
        after = jnp.where(first, arriving[block], arriving[1 - block])
        for part in range(half // LANES):
            lanes = slice(part * LANES, (part + 1) * LANES)
            start = before[part : part + 1]
            state = ls_ref[:, lanes] + cum_ref[:, lanes] * start
            if block == 0:
                out_ref[:, lanes] = state.astype(BF16)
            else:
                send_ref[:, lanes] = state
            previous = jnp.where(row == 0, start, pltpu.roll(state, 1, 0))
            adjoint = la_ref[:, lanes] + pc_ref[:, lanes] * after[part : part + 1]
            dpre_ref[there, lanes] = (adjoint * (k1_ref[:, lanes] * previous + k2_ref[:, lanes])).astype(BF16)
            far = slice(half + part * LANES, half + (part + 1) * LANES)
            dpre_ref[there, far] = (adjoint * k3_ref[:, lanes]).astype(BF16)
            direct_ref[there, lanes] = adjoint * k4_ref[:, lanes]
        weight_grad = weight_grad + lax.dot_general(
            x_ref[...], dpre_ref[there, :], (((0,), (0,)), ((), ())), preferred_element_type=F32
        )
    depth = SUB // 2
    low = lax.broadcasted_iota(jnp.int32, (SUB, 2 * half), 0) < depth
    for i in range(n_x):
        for pair in range(n_z // 2):
            u = weight_grad[i * 2 * n_z * depth + pair * SUB :][:SUB]
            v = weight_grad[(i * 2 + 1) * n_z * depth + pair * SUB :][:SUB]
            gw_ref[i * n_z + 2 * pair] = jnp.where(low, u, pltpu.roll(v, depth, 0))
            gw_ref[i * n_z + 2 * pair + 1] = jnp.where(low, pltpu.roll(u, depth, 0), v)


def inputs_kernel(dpre_ref, direct_ref, w_ref, states_ref, gx_ref, send_ref):
    rows = gx_ref.shape[0]
    core = lax.axis_index("core")
    back = lax.dot_general(dpre_ref[...], w_ref[core], (((1,), (1,)), ((), ())), preferred_element_type=F32)
    total = direct_ref[...] + back
    gx_ref[...] = total[:rows].astype(BF16)
    send_ref[:rows] = states_ref[...]
    send_ref[rows:] = total[rows:]


def unswap_kernel(out_ref, gx_ref, got_ref, outputs_ref, grad_ref, order_ref):
    rows, half = out_ref.shape
    first = lax.axis_index("core") == 0
    for r, (own, whole) in enumerate(((out_ref, outputs_ref), (gx_ref, grad_ref))):
        mine = own[...].astype(F32)
        got = got_ref[r * rows : (r + 1) * rows]
        whole[:, :half] = jnp.where(first, mine, got).astype(BF16)
        whole[:, half:] = jnp.where(first, got, mine).astype(BF16)
    order_ref[...] = jnp.zeros_like(order_ref)


def sum_kernel(pieces_ref, _, keep_ref, send_ref):
    total = pieces_ref[0]
    for j in range(1, pieces_ref.shape[0]):
        total = total + pieces_ref[j]
    first = lax.axis_index("core") == 0
    depth = SUB // 2
    keep_ref[...] = jnp.where(first, total[:depth], total[depth:])
    send_ref[...] = jnp.where(first, total[depth:], total[:depth])


def join_kernel(keep_ref, got_ref, grad_ref):
    first = lax.axis_index("core") == 0
    keep, got = keep_ref[...], got_ref[...]
    grad_ref[:, 0, :] = jnp.where(first, keep, got)
    grad_ref[:, 1, :] = jnp.where(first, got, keep)


def per_device(inputs, doc_start, gate_weight, gate_bias, decay_rate, cotangent):
    _, rows, width = inputs.shape
    head_dim, heads, wide = gate_weight.shape
    n_x, n_z = lax.axis_size("x"), lax.axis_size("z")
    chips = n_x * n_z
    half = width // 2
    depth = SUB // 2
    shape = jax.ShapeDtypeStruct
    vmem = pl.BlockSpec(memory_space=pltpu.VMEM)

    def call(kernel, operands, outs, name, scratch=(), cost=None):
        return pl.pallas_call(
            kernel,
            out_shape=outs,
            in_specs=[vmem] * len(operands),
            scratch_shapes=scratch,
            compiler_params=pltpu.CompilerParams(vmem_limit_bytes=16 << 20),
            cost_estimate=cost,
            name=name,
        )(*operands)

    swap = lambda value: lax.ppermute(value, "core", [(0, 1), (1, 0)])
    packed = shape((2 * rows + SUB, half), F32)
    gates = (jnp.moveaxis(gate_weight, 1, 0), gate_bias, decay_rate.reshape(1, width))
    cost = pl.CostEstimate(flops=4 * 10**9, bytes_accessed=4096, transcendentals=0)
    order = call(head_kernel, (), shape((SUB, LANES), F32), "head", cost=cost)
    operands = (inputs.reshape(rows, width), cotangent.reshape(rows, width), doc_start, *gates[1:], order)
    send, own = call(pack_kernel, operands, [packed] * 2, "pack")
    got = swap(send)
    fields = [shape((rows, half), BF16)] + [shape((rows, half), F32)] * 8
    tiles = half // LANES
    summary, *own = call(own_kernel, (own, *gates), [shape((3, tiles, LANES), F32)] + fields, "own_scans")
    summary, *got = call(got_kernel, (got, *gates, summary), [shape((3, 2 * tiles, LANES), F32)] + fields, "got_scans")
    met = lax.ppermute(order, "z", [(i, i ^ 1) for i in range(n_z)])
    spread = call(spread_kernel, (summary, met), shape((chips, 3, 2 * tiles, LANES), F32), "spread")
    everyone = lax.all_to_all(spread, ("x", "z"), 0, 0)
    out, states, dpre, direct, gw = call(
        lambda *refs: finish_kernel(n_x, n_z, *refs),
        (everyone, *own, *got),
        [
            shape((rows, half), BF16),
            shape((rows, half), F32),
            shape((2 * rows, wide), BF16),
            shape((2 * rows, half), F32),
            shape((chips, SUB, wide), F32),
        ],
        "finish",
    )
    pieces = lax.all_to_all(gw, ("x", "z"), 0, 0)
    gx, send = call(
        inputs_kernel, (dpre, direct, gates[0], states), [shape((rows, half), BF16), shape((2 * rows, half), F32)], "grad_inputs"
    )
    outputs, grad_inputs, order = call(
        unswap_kernel, (out, gx, swap(send)), [shape((rows, width), BF16)] * 2 + [shape((SUB, LANES), F32)], "unswap"
    )
    keep, give = call(sum_kernel, (pieces, order), [shape((depth, wide), F32)] * 2, "sum")
    grad_gate_weight = call(join_kernel, (keep, swap(give)), shape((depth, heads, wide), F32), "join")
    return (outputs[None], grad_inputs[None], grad_gate_weight)


def solution(mesh):
    n_dp, n_ctx, n_mp = mesh.devices.shape
    fine = Mesh(mesh.devices.reshape(n_dp // 2, 2, n_ctx, n_mp), ("x", "core", "z", "mp"))
    place = ("x", "core", "z")
    return jax.shard_map(
        per_device,
        mesh=fine,
        in_specs=(P(None, place, "mp"), P(None, place), P(None, "mp", None), P("mp", None), P("mp"), P(None, place, "mp")),
        out_specs=(P(None, place, "mp"), P(None, place, "mp"), P(place, "mp", None)),
        check_vma=False,
    )
```

```python
import jax
import jax.numpy as jnp
from jax import lax
from jax.experimental import pallas as pl
from jax.experimental.pallas import tpu as pltpu
from jax.sharding import Mesh, PartitionSpec as P

LANES = 128
SUB = 8
F32 = jnp.float32
BF16 = jnp.bfloat16


def column_scan(decays, drives, backward):
    rows = decays.shape[0]
    groups = rows // SUB
    a = decays.reshape(groups, SUB, LANES)
    b = drives.reshape(groups, SUB, LANES)
    place = lax.broadcasted_iota(jnp.int32, (groups, SUB, LANES), 1)
    step = 1
    while step < SUB:
        if backward:
            shift, ok = SUB - step, place < SUB - step
        else:
            shift, ok = step, place >= step
        a_far = jnp.where(ok, pltpu.roll(a, shift, 1), 1.0)
        b_far = jnp.where(ok, pltpu.roll(b, shift, 1), 0.0)
        b = a * b_far + b
        a = a * a_far
        step *= 2
    order = range(groups - 1, -1, -1) if backward else range(groups)
    edge = 0 if backward else SUB - 1
    a_in = jnp.ones((1, LANES), F32)
    b_in = jnp.zeros((1, LANES), F32)
    a_out, b_out = [None] * groups, [None] * groups
    for g in order:
        a_out[g] = a[g] * a_in
        b_out[g] = a[g] * b_in + b[g]
        a_in = a_out[g][edge : edge + 1]
        b_in = b_out[g][edge : edge + 1]
    return jnp.concatenate(a_out, 0), jnp.concatenate(b_out, 0), a_in, b_in


def head_kernel(order_ref):
    order_ref[...] = jnp.zeros_like(order_ref)


def pack_kernel(x_ref, cot_ref, doc_ref, bias_ref, rate_ref, order_ref, send_ref, own_ref):
    rows, width = x_ref.shape
    half = width // 2
    first = lax.axis_index("core") == 0
    for r, ref in enumerate((x_ref, cot_ref)):
        both = ref[...].astype(F32)
        send_ref[r * rows : (r + 1) * rows, :] = jnp.where(first, both[:, half:], both[:, :half])
        own_ref[r * rows : (r + 1) * rows, :] = jnp.where(first, both[:, :half], both[:, half:])
    doc = jnp.broadcast_to(doc_ref[...].astype(F32), (SUB, rows))
    doc = jnp.concatenate([doc] * (half // rows), axis=1)
    send_ref[2 * rows : 2 * rows + SUB, :] = doc
    own_ref[2 * rows : 2 * rows + SUB, :] = doc


def local_scans(pack_ref, w_ref, bias_ref, rate_ref, x_ref, k1_ref, k2_ref, k3_ref, k4_ref, cum_ref, ls_ref, pc_ref, la_ref):
    rows, half = x_ref.shape
    core = lax.axis_index("core")
    row = lax.broadcasted_iota(jnp.int32, (rows, LANES), 0)
    x_ref[...] = pack_ref[:rows].astype(BF16)
    rate8 = -8.0 * jnp.where(core == 0, rate_ref[:, :half], rate_ref[:, half:])
    pre = jnp.dot(x_ref[...], w_ref[core], preferred_element_type=F32) + bias_ref[pl.ds(core, 1), :]
    keep = 1.0 - jnp.transpose(jnp.broadcast_to(pack_ref[2 * rows : 2 * rows + 1, :rows], (LANES, rows)))
    kept = keep > 0.5
    ends = []
    for part in range(half // LANES):
        lanes = slice(part * LANES, (part + 1) * LANES)
        rgate = jax.nn.sigmoid(pre[:, lanes])
        igate = jax.nn.sigmoid(pre[:, half + part * LANES : half + (part + 1) * LANES])
        x = pack_ref[:rows, lanes]
        rate = rate8[:, lanes]
        decay = jnp.exp(rate * rgate)
        carry = decay * keep
        square = decay * decay
        root = jnp.sqrt(1.0 - square + 0.01)
        scale = jnp.where(kept, root, 1.0)
        dscale = jnp.where(kept, -square / root, 0.0)
        slope = rate * (rgate * (1.0 - rgate))
        k4 = scale * igate
        drive = k4 * x
        k1_ref[:, lanes] = carry * slope
        k2_ref[:, lanes] = igate * x * dscale * slope
        k3_ref[:, lanes] = drive * (1.0 - igate)
        k4_ref[:, lanes] = k4
        cum, state, product, last = column_scan(carry, drive, False)
        cum_ref[:, lanes] = cum
        ls_ref[:, lanes] = state
        ahead = jnp.where(row == rows - 1, 1.0, pltpu.roll(carry, rows - 1, 0))
        pc, adjoint, _, top = column_scan(ahead, pack_ref[rows : 2 * rows, lanes], True)
        pc_ref[:, lanes] = pc
        la_ref[:, lanes] = adjoint
        ends.append((product, last, carry[0:1] * top))
    return ends


def own_kernel(pack_ref, w_ref, bias_ref, rate_ref, summary_ref, *refs):
    for part, values in enumerate(local_scans(pack_ref, w_ref, bias_ref, rate_ref, *refs)):
        for i, value in enumerate(values):
            summary_ref[i, part : part + 1, :] = value


def got_kernel(pack_ref, w_ref, bias_ref, rate_ref, own_ref, spread_ref, *refs):
    *refs, summary_ref = refs
    core = lax.axis_index("core")
    ends = local_scans(pack_ref, w_ref, bias_ref, rate_ref, *refs)
    for part, values in enumerate(ends):
        for i, value in enumerate(values):
            summary_ref[i, pl.ds(core * len(ends) + part, 1), :] = own_ref[i, part : part + 1, :]
            summary_ref[i, pl.ds((1 - core) * len(ends) + part, 1), :] = value
    summary = summary_ref[...]
    for j in range(spread_ref.shape[0]):
        spread_ref[j] = summary


def fold(all_ref, order, kind, wanted=None):
    product = jnp.ones(all_ref.shape[2:], F32)
    value = jnp.zeros(all_ref.shape[2:], F32)
    for z in order:
        a, b = all_ref[z, 0], all_ref[z, kind]
        if wanted is not None:
            a, b = jnp.where(wanted(z), a, 1.0), jnp.where(wanted(z), b, 0.0)
        value = a * value + b
        product = product * a
    return product, value


def totals_kernel(all_ref, totals_ref):
    n_z = all_ref.shape[0]
    totals_ref[0], totals_ref[1] = fold(all_ref, range(n_z), 1)
    totals_ref[2] = fold(all_ref, range(n_z - 1, -1, -1), 2)[1]


def edges(all_ref, rows, own, kind, x, z, backward):
    n_x, n_z = len(rows), all_ref.shape[0]
    half = all_ref.shape[2] // 2
    cores = (slice(0, half), slice(half, 2 * half))
    near, far = (cores[1], cores[0]) if backward else cores
    order = range(n_z - 1, -1, -1) if backward else range(n_z)
    apply = lambda link, at, value: link[0][at] * value + link[1][at]
    carried = jnp.zeros((half, LANES), F32)
    for i in range(n_x - 1, 0, -1) if backward else range(n_x - 1):
        link = rows[i][0], rows[i][kind]
        carried = jnp.where(i > x if backward else i < x, apply(link, far, apply(link, near, carried)), carried)
    partial = fold(all_ref, order, kind, (lambda i: i > z) if backward else (lambda i: i < z))
    ahead = apply(partial, near, carried)
    behind = apply(partial, far, apply((own[0], own[kind]), near, carried))
    return (behind, ahead) if backward else (ahead, behind)


def finish_kernel(n_x, n_z, all_ref, *refs):
    row_refs, refs = refs[:n_x], refs[n_x:]
    own, got, (out_ref, send_ref, dpre_ref, direct_ref, gw_ref) = refs[:9], refs[9:18], refs[18:]
    rows, half = out_ref.shape
    first = lax.axis_index("core") == 0
    at_x, at_z = lax.axis_index("x"), lax.axis_index("z")
    totals = [ref[...] for ref in row_refs]
    ordered = []
    for i in range(n_x):
        here = totals[0]
        for d in range(1, n_x):
            here = jnp.where((at_x ^ d) == i, totals[d], here)
        ordered.append(here)
    entering = edges(all_ref, ordered, totals[0], 1, at_x, at_z, False)
    arriving = edges(all_ref, ordered, totals[0], 2, at_x, at_z, True)
    row = lax.broadcasted_iota(jnp.int32, (rows, LANES), 0)
    weight_grad = 0.0
    for block, (x_ref, k1_ref, k2_ref, k3_ref, k4_ref, cum_ref, ls_ref, pc_ref, la_ref) in enumerate((own, got)):
        there = slice(block * rows, (block + 1) * rows)
        before = jnp.where(first, entering[block], entering[1 - block])
        after = jnp.where(first, arriving[block], arriving[1 - block])
        for part in range(half // LANES):
            lanes = slice(part * LANES, (part + 1) * LANES)
            start = before[part : part + 1]
            state = ls_ref[:, lanes] + cum_ref[:, lanes] * start
            if block == 0:
                out_ref[:, lanes] = state.astype(BF16)
            else:
                send_ref[:, lanes] = state
            previous = jnp.where(row == 0, start, pltpu.roll(state, 1, 0))
            adjoint = la_ref[:, lanes] + pc_ref[:, lanes] * after[part : part + 1]
            dpre_ref[there, lanes] = (adjoint * (k1_ref[:, lanes] * previous + k2_ref[:, lanes])).astype(BF16)
            far = slice(half + part * LANES, half + (part + 1) * LANES)
            dpre_ref[there, far] = (adjoint * k3_ref[:, lanes]).astype(BF16)
            direct_ref[there, lanes] = adjoint * k4_ref[:, lanes]
        weight_grad = weight_grad + lax.dot_general(
            x_ref[...], dpre_ref[there, :], (((0,), (0,)), ((), ())), preferred_element_type=F32
        )
    depth = SUB // 2
    low = lax.broadcasted_iota(jnp.int32, (SUB, 2 * half), 0) < depth
    for i in range(n_x):
        for pair in range(n_z // 2):
            u = weight_grad[i * 2 * n_z * depth + pair * SUB :][:SUB]
            v = weight_grad[(i * 2 + 1) * n_z * depth + pair * SUB :][:SUB]
            gw_ref[i * n_z + 2 * pair] = jnp.where(low, u, pltpu.roll(v, depth, 0))
            gw_ref[i * n_z + 2 * pair + 1] = jnp.where(low, pltpu.roll(u, depth, 0), v)


def inputs_kernel(dpre_ref, direct_ref, w_ref, states_ref, gx_ref, send_ref):
    rows = gx_ref.shape[0]
    core = lax.axis_index("core")
    back = lax.dot_general(dpre_ref[...], w_ref[core], (((1,), (1,)), ((), ())), preferred_element_type=F32)
    total = direct_ref[...] + back
    gx_ref[...] = total[:rows].astype(BF16)
    send_ref[:rows] = states_ref[...]
    send_ref[rows:] = total[rows:]


def unswap_kernel(out_ref, gx_ref, got_ref, outputs_ref, grad_ref, order_ref):
    rows, half = out_ref.shape
    first = lax.axis_index("core") == 0
    for r, (own, whole) in enumerate(((out_ref, outputs_ref), (gx_ref, grad_ref))):
        mine = own[...].astype(F32)
        got = got_ref[r * rows : (r + 1) * rows]
        whole[:, :half] = jnp.where(first, mine, got).astype(BF16)
        whole[:, half:] = jnp.where(first, got, mine).astype(BF16)
    order_ref[...] = jnp.zeros_like(order_ref)


def sum_kernel(pieces_ref, _, keep_ref, send_ref):
    total = pieces_ref[0]
    for j in range(1, pieces_ref.shape[0]):
        total = total + pieces_ref[j]
    first = lax.axis_index("core") == 0
    depth = SUB // 2
    keep_ref[...] = jnp.where(first, total[:depth], total[depth:])
    send_ref[...] = jnp.where(first, total[depth:], total[:depth])


def join_kernel(keep_ref, got_ref, grad_ref):
    first = lax.axis_index("core") == 0
    keep, got = keep_ref[...], got_ref[...]
    grad_ref[:, 0, :] = jnp.where(first, keep, got)
    grad_ref[:, 1, :] = jnp.where(first, got, keep)


def per_device(inputs, doc_start, gate_weight, gate_bias, decay_rate, cotangent):
    _, rows, width = inputs.shape
    head_dim, heads, wide = gate_weight.shape
    n_x, n_z = lax.axis_size("x"), lax.axis_size("z")
    chips = n_x * n_z
    half = width // 2
    depth = SUB // 2
    shape = jax.ShapeDtypeStruct
    vmem = pl.BlockSpec(memory_space=pltpu.VMEM)

    def call(kernel, operands, outs, name, scratch=(), cost=None):
        return pl.pallas_call(
            kernel,
            out_shape=outs,
            in_specs=[vmem] * len(operands),
            scratch_shapes=scratch,
            compiler_params=pltpu.CompilerParams(vmem_limit_bytes=16 << 20),
            cost_estimate=cost,
            name=name,
        )(*operands)

    swap = lambda value: lax.ppermute(value, "core", [(0, 1), (1, 0)])
    packed = shape((2 * rows + SUB, half), F32)
    gates = (jnp.moveaxis(gate_weight, 1, 0), gate_bias, decay_rate.reshape(1, width))
    cost = pl.CostEstimate(flops=4 * 10**9, bytes_accessed=4096, transcendentals=0)
    order = call(head_kernel, (), shape((SUB, LANES), F32), "head", cost=cost)
    operands = (inputs.reshape(rows, width), cotangent.reshape(rows, width), doc_start, *gates[1:], order)
    send, own = call(pack_kernel, operands, [packed] * 2, "pack")
    got = swap(send)
    fields = [shape((rows, half), BF16)] + [shape((rows, half), F32)] * 8
    tiles = half // LANES
    summary, *own = call(own_kernel, (own, *gates), [shape((3, tiles, LANES), F32)] + fields, "own_scans")
    spread, *got = call(
        got_kernel,
        (got, *gates, summary),
        [shape((n_z, 3, 2 * tiles, LANES), F32)] + fields,
        "got_scans",
        [pltpu.VMEM((3, 2 * tiles, LANES), F32)],
    )
    row = lax.all_to_all(spread, "z", 0, 0)
    totals = call(totals_kernel, (row,), shape((3, 2 * tiles, LANES), F32), "totals")
    rows_x = [totals] + [lax.ppermute(totals, "x", [(i, i ^ d) for i in range(n_x)]) for d in range(1, n_x)]
    out, states, dpre, direct, gw = call(
        lambda *refs: finish_kernel(n_x, n_z, *refs),
        (row, *rows_x, *own, *got),
        [
            shape((rows, half), BF16),
            shape((rows, half), F32),
            shape((2 * rows, wide), BF16),
            shape((2 * rows, half), F32),
            shape((chips, SUB, wide), F32),
        ],
        "finish",
    )
    pieces = lax.all_to_all(gw, ("x", "z"), 0, 0)
    gx, send = call(
        inputs_kernel, (dpre, direct, gates[0], states), [shape((rows, half), BF16), shape((2 * rows, half), F32)], "grad_inputs"
    )
    outputs, grad_inputs, order = call(
        unswap_kernel, (out, gx, swap(send)), [shape((rows, width), BF16)] * 2 + [shape((SUB, LANES), F32)], "unswap"
    )
    keep, give = call(sum_kernel, (pieces, order), [shape((depth, wide), F32)] * 2, "sum")
    grad_gate_weight = call(join_kernel, (keep, swap(give)), shape((depth, heads, wide), F32), "join")
    return (outputs[None], grad_inputs[None], grad_gate_weight)


def solution(mesh):
    n_dp, n_ctx, n_mp = mesh.devices.shape
    fine = Mesh(mesh.devices.reshape(n_dp // 2, 2, n_ctx, n_mp), ("x", "core", "z", "mp"))
    place = ("x", "core", "z")
    return jax.shard_map(
        per_device,
        mesh=fine,
        in_specs=(P(None, place, "mp"), P(None, place), P(None, "mp", None), P("mp", None), P("mp"), P(None, place, "mp")),
        out_specs=(P(None, place, "mp"), P(None, place, "mp"), P(place, "mp", None)),
        check_vma=False,
    )
```

```python
import jax
import jax.numpy as jnp
from jax import lax
from jax.experimental import pallas as pl
from jax.experimental.pallas import tpu as pltpu
from jax.sharding import Mesh, PartitionSpec as P

LANES = 128
SUB = 8
F32 = jnp.float32
BF16 = jnp.bfloat16


def column_scan(decays, drives, backward):
    rows = decays.shape[0]
    groups = rows // SUB
    a = decays.reshape(groups, SUB, LANES)
    b = drives.reshape(groups, SUB, LANES)
    place = lax.broadcasted_iota(jnp.int32, (groups, SUB, LANES), 1)
    step = 1
    while step < SUB:
        if backward:
            shift, ok = SUB - step, place < SUB - step
        else:
            shift, ok = step, place >= step
        a_far = jnp.where(ok, pltpu.roll(a, shift, 1), 1.0)
        b_far = jnp.where(ok, pltpu.roll(b, shift, 1), 0.0)
        b = a * b_far + b
        a = a * a_far
        step *= 2
    order = range(groups - 1, -1, -1) if backward else range(groups)
    edge = 0 if backward else SUB - 1
    a_in = jnp.ones((1, LANES), F32)
    b_in = jnp.zeros((1, LANES), F32)
    a_out, b_out = [None] * groups, [None] * groups
    for g in order:
        a_out[g] = a[g] * a_in
        b_out[g] = a[g] * b_in + b[g]
        a_in = a_out[g][edge : edge + 1]
        b_in = b_out[g][edge : edge + 1]
    return jnp.concatenate(a_out, 0), jnp.concatenate(b_out, 0), a_in, b_in


def head_kernel(order_ref):
    order_ref[...] = jnp.zeros_like(order_ref)


def pack_kernel(x_ref, cot_ref, doc_ref, bias_ref, rate_ref, order_ref, send_ref, own_ref):
    rows, width = x_ref.shape
    half = width // 2
    first = lax.axis_index("core") == 0
    for r, ref in enumerate((x_ref, cot_ref)):
        both = ref[...].astype(F32)
        send_ref[r * rows : (r + 1) * rows, :] = jnp.where(first, both[:, half:], both[:, :half])
        own_ref[r * rows : (r + 1) * rows, :] = jnp.where(first, both[:, :half], both[:, half:])
    doc = jnp.broadcast_to(doc_ref[...].astype(F32), (SUB, rows))
    doc = jnp.concatenate([doc] * (half // rows), axis=1)
    send_ref[2 * rows : 2 * rows + SUB, :] = doc
    own_ref[2 * rows : 2 * rows + SUB, :] = doc


def local_scans(pack_ref, w_ref, bias_ref, rate_ref, x_ref, k1_ref, k2_ref, k3_ref, k4_ref, cum_ref, ls_ref, pc_ref, la_ref):
    rows, half = x_ref.shape
    core = lax.axis_index("core")
    row = lax.broadcasted_iota(jnp.int32, (rows, LANES), 0)
    x_ref[...] = pack_ref[:rows].astype(BF16)
    rate8 = -8.0 * jnp.where(core == 0, rate_ref[:, :half], rate_ref[:, half:])
    pre = jnp.dot(x_ref[...], w_ref[core], preferred_element_type=F32) + bias_ref[pl.ds(core, 1), :]
    keep = 1.0 - jnp.transpose(jnp.broadcast_to(pack_ref[2 * rows : 2 * rows + 1, :rows], (LANES, rows)))
    kept = keep > 0.5
    ends = []
    for part in range(half // LANES):
        lanes = slice(part * LANES, (part + 1) * LANES)
        rgate = jax.nn.sigmoid(pre[:, lanes])
        igate = jax.nn.sigmoid(pre[:, half + part * LANES : half + (part + 1) * LANES])
        x = pack_ref[:rows, lanes]
        rate = rate8[:, lanes]
        decay = jnp.exp(rate * rgate)
        carry = decay * keep
        square = decay * decay
        floored = 1.0 - square + 0.01
        inverse = lax.rsqrt(floored)
        scale = jnp.where(kept, floored * inverse, 1.0)
        dscale = jnp.where(kept, -square * inverse, 0.0)
        slope = rate * (rgate * (1.0 - rgate))
        k4 = scale * igate
        drive = k4 * x
        k1_ref[:, lanes] = carry * slope
        k2_ref[:, lanes] = igate * x * dscale * slope
        k3_ref[:, lanes] = drive * (1.0 - igate)
        k4_ref[:, lanes] = k4
        cum, state, product, last = column_scan(carry, drive, False)
        cum_ref[:, lanes] = cum
        ls_ref[:, lanes] = state
        ahead = jnp.where(row == rows - 1, 1.0, pltpu.roll(carry, rows - 1, 0))
        pc, adjoint, _, top = column_scan(ahead, pack_ref[rows : 2 * rows, lanes], True)
        pc_ref[:, lanes] = pc
        la_ref[:, lanes] = adjoint
        ends.append((product, last, carry[0:1] * top))
    return ends


def own_kernel(pack_ref, w_ref, bias_ref, rate_ref, summary_ref, *refs):
    for part, values in enumerate(local_scans(pack_ref, w_ref, bias_ref, rate_ref, *refs)):
        for i, value in enumerate(values):
            summary_ref[i, part : part + 1, :] = value


def got_kernel(pack_ref, w_ref, bias_ref, rate_ref, own_ref, summary_ref, *refs):
    core = lax.axis_index("core")
    ends = local_scans(pack_ref, w_ref, bias_ref, rate_ref, *refs)
    for part, values in enumerate(ends):
        for i, value in enumerate(values):
            summary_ref[i, pl.ds(core * len(ends) + part, 1), :] = own_ref[i, part : part + 1, :]
            summary_ref[i, pl.ds((1 - core) * len(ends) + part, 1), :] = value


def spread_kernel(summary_ref, _, spread_ref):
    summary = summary_ref[...]
    for j in range(spread_ref.shape[0]):
        spread_ref[j] = summary


def fold(all_ref, order, kind, base, wanted=None):
    product = jnp.ones(all_ref.shape[2:], F32)
    value = jnp.zeros(all_ref.shape[2:], F32)
    for z in order:
        a, b = all_ref[base + z, 0], all_ref[base + z, kind]
        if wanted is not None:
            a, b = jnp.where(wanted(z), a, 1.0), jnp.where(wanted(z), b, 0.0)
        value = a * value + b
        product = product * a
    return product, value


def edges(all_ref, kind, x, z, n_x, n_z, backward):
    half = all_ref.shape[2] // 2
    cores = (slice(0, half), slice(half, 2 * half))
    near, far = (cores[1], cores[0]) if backward else cores
    order = range(n_z - 1, -1, -1) if backward else range(n_z)
    apply = lambda link, at, value: link[0][at] * value + link[1][at]
    carried = jnp.zeros((half, LANES), F32)
    for i in range(n_x - 1, 0, -1) if backward else range(n_x - 1):
        link = fold(all_ref, order, kind, i * n_z)
        carried = jnp.where(i > x if backward else i < x, apply(link, far, apply(link, near, carried)), carried)
    base = x * n_z
    whole = fold(all_ref, order, kind, base)
    partial = fold(all_ref, order, kind, base, (lambda i: i > z) if backward else (lambda i: i < z))
    ahead = apply(partial, near, carried)
    behind = apply(partial, far, apply(whole, near, carried))
    return (behind, ahead) if backward else (ahead, behind)


def finish_kernel(n_x, n_z, all_ref, *refs):
    own, got, (out_ref, send_ref, dpre_ref, direct_ref, gw_ref) = refs[:9], refs[9:18], refs[18:]
    rows, half = out_ref.shape
    first = lax.axis_index("core") == 0
    at_x, at_z = lax.axis_index("x"), lax.axis_index("z")
    entering = edges(all_ref, 1, at_x, at_z, n_x, n_z, False)
    arriving = edges(all_ref, 2, at_x, at_z, n_x, n_z, True)
    row = lax.broadcasted_iota(jnp.int32, (rows, LANES), 0)
    weight_grad = 0.0
    for block, (x_ref, k1_ref, k2_ref, k3_ref, k4_ref, cum_ref, ls_ref, pc_ref, la_ref) in enumerate((own, got)):
        there = slice(block * rows, (block + 1) * rows)
        before = jnp.where(first, entering[block], entering[1 - block])
        after = jnp.where(first, arriving[block], arriving[1 - block])
        for part in range(half // LANES):
            lanes = slice(part * LANES, (part + 1) * LANES)
            start = before[part : part + 1]
            state = ls_ref[:, lanes] + cum_ref[:, lanes] * start
            if block == 0:
                out_ref[:, lanes] = state.astype(BF16)
            else:
                send_ref[:, lanes] = state
            previous = jnp.where(row == 0, start, pltpu.roll(state, 1, 0))
            adjoint = la_ref[:, lanes] + pc_ref[:, lanes] * after[part : part + 1]
            dpre_ref[there, lanes] = (adjoint * (k1_ref[:, lanes] * previous + k2_ref[:, lanes])).astype(BF16)
            far = slice(half + part * LANES, half + (part + 1) * LANES)
            dpre_ref[there, far] = (adjoint * k3_ref[:, lanes]).astype(BF16)
            direct_ref[there, lanes] = adjoint * k4_ref[:, lanes]
        weight_grad = weight_grad + lax.dot_general(
            x_ref[...], dpre_ref[there, :], (((0,), (0,)), ((), ())), preferred_element_type=F32
        )
    depth = SUB // 2
    low = lax.broadcasted_iota(jnp.int32, (SUB, 2 * half), 0) < depth
    for i in range(n_x):
        for pair in range(n_z // 2):
            u = weight_grad[i * 2 * n_z * depth + pair * SUB :][:SUB]
            v = weight_grad[(i * 2 + 1) * n_z * depth + pair * SUB :][:SUB]
            gw_ref[i * n_z + 2 * pair] = jnp.where(low, u, pltpu.roll(v, depth, 0))
            gw_ref[i * n_z + 2 * pair + 1] = jnp.where(low, pltpu.roll(u, depth, 0), v)


def inputs_kernel(dpre_ref, direct_ref, w_ref, states_ref, gx_ref, send_ref):
    rows = gx_ref.shape[0]
    core = lax.axis_index("core")
    back = lax.dot_general(dpre_ref[...], w_ref[core], (((1,), (1,)), ((), ())), preferred_element_type=F32)
    total = direct_ref[...] + back
    gx_ref[...] = total[:rows].astype(BF16)
    send_ref[:rows] = states_ref[...]
    send_ref[rows:] = total[rows:]


def unswap_kernel(out_ref, gx_ref, got_ref, outputs_ref, grad_ref, order_ref):
    rows, half = out_ref.shape
    first = lax.axis_index("core") == 0
    for r, (own, whole) in enumerate(((out_ref, outputs_ref), (gx_ref, grad_ref))):
        mine = own[...].astype(F32)
        got = got_ref[r * rows : (r + 1) * rows]
        whole[:, :half] = jnp.where(first, mine, got).astype(BF16)
        whole[:, half:] = jnp.where(first, got, mine).astype(BF16)
    order_ref[...] = jnp.zeros_like(order_ref)


def sum_kernel(pieces_ref, _, keep_ref, send_ref):
    total = pieces_ref[0]
    for j in range(1, pieces_ref.shape[0]):
        total = total + pieces_ref[j]
    first = lax.axis_index("core") == 0
    depth = SUB // 2
    keep_ref[...] = jnp.where(first, total[:depth], total[depth:])
    send_ref[...] = jnp.where(first, total[depth:], total[:depth])


def join_kernel(keep_ref, got_ref, grad_ref):
    first = lax.axis_index("core") == 0
    keep, got = keep_ref[...], got_ref[...]
    grad_ref[:, 0, :] = jnp.where(first, keep, got)
    grad_ref[:, 1, :] = jnp.where(first, got, keep)


def per_device(inputs, doc_start, gate_weight, gate_bias, decay_rate, cotangent):
    _, rows, width = inputs.shape
    head_dim, heads, wide = gate_weight.shape
    n_x, n_z = lax.axis_size("x"), lax.axis_size("z")
    chips = n_x * n_z
    half = width // 2
    depth = SUB // 2
    shape = jax.ShapeDtypeStruct
    vmem = pl.BlockSpec(memory_space=pltpu.VMEM)

    def call(kernel, operands, outs, name, scratch=(), cost=None):
        return pl.pallas_call(
            kernel,
            out_shape=outs,
            in_specs=[vmem] * len(operands),
            scratch_shapes=scratch,
            compiler_params=pltpu.CompilerParams(vmem_limit_bytes=16 << 20),
            cost_estimate=cost,
            name=name,
        )(*operands)

    swap = lambda value: lax.ppermute(value, "core", [(0, 1), (1, 0)])
    packed = shape((2 * rows + SUB, half), F32)
    gates = (jnp.moveaxis(gate_weight, 1, 0), gate_bias, decay_rate.reshape(1, width))
    cost = pl.CostEstimate(flops=4 * 10**9, bytes_accessed=4096, transcendentals=0)
    order = call(head_kernel, (), shape((SUB, LANES), F32), "head", cost=cost)
    operands = (inputs.reshape(rows, width), cotangent.reshape(rows, width), doc_start, *gates[1:], order)
    send, own = call(pack_kernel, operands, [packed] * 2, "pack")
    got = swap(send)
    fields = [shape((rows, half), BF16)] + [shape((rows, half), F32)] * 8
    tiles = half // LANES
    summary, *own = call(own_kernel, (own, *gates), [shape((3, tiles, LANES), F32)] + fields, "own_scans")
    summary, *got = call(got_kernel, (got, *gates, summary), [shape((3, 2 * tiles, LANES), F32)] + fields, "got_scans")
    met = lax.ppermute(order, "z", [(i, i ^ 1) for i in range(n_z)])
    spread = call(spread_kernel, (summary, met), shape((chips, 3, 2 * tiles, LANES), F32), "spread")
    everyone = lax.all_to_all(spread, ("x", "z"), 0, 0)
    out, states, dpre, direct, gw = call(
        lambda *refs: finish_kernel(n_x, n_z, *refs),
        (everyone, *own, *got),
        [
            shape((rows, half), BF16),
            shape((rows, half), F32),
            shape((2 * rows, wide), BF16),
            shape((2 * rows, half), F32),
            shape((chips, SUB, wide), F32),
        ],
        "finish",
    )
    pieces = lax.all_to_all(gw, ("x", "z"), 0, 0)
    gx, send = call(
        inputs_kernel, (dpre, direct, gates[0], states), [shape((rows, half), BF16), shape((2 * rows, half), F32)], "grad_inputs"
    )
    outputs, grad_inputs, order = call(
        unswap_kernel, (out, gx, swap(send)), [shape((rows, width), BF16)] * 2 + [shape((SUB, LANES), F32)], "unswap"
    )
    keep, give = call(sum_kernel, (pieces, order), [shape((depth, wide), F32)] * 2, "sum")
    grad_gate_weight = call(join_kernel, (keep, swap(give)), shape((depth, heads, wide), F32), "join")
    return (outputs[None], grad_inputs[None], grad_gate_weight)


def solution(mesh):
    n_dp, n_ctx, n_mp = mesh.devices.shape
    fine = Mesh(mesh.devices.reshape(n_dp // 2, 2, n_ctx, n_mp), ("x", "core", "z", "mp"))
    place = ("x", "core", "z")
    return jax.shard_map(
        per_device,
        mesh=fine,
        in_specs=(P(None, place, "mp"), P(None, place), P(None, "mp", None), P("mp", None), P("mp"), P(None, place, "mp")),
        out_specs=(P(None, place, "mp"), P(None, place, "mp"), P(place, "mp", None)),
        check_vma=False,
    )
```

```python
import jax
import jax.numpy as jnp
from jax import lax
from jax.experimental import pallas as pl
from jax.experimental.pallas import tpu as pltpu
from jax.sharding import Mesh, PartitionSpec as P

LANES = 128
SUB = 8
F32 = jnp.float32
BF16 = jnp.bfloat16


def column_scan(decays, drives, backward):
    rows = decays.shape[0]
    groups = rows // SUB
    a = decays.reshape(groups, SUB, LANES)
    b = drives.reshape(groups, SUB, LANES)
    place = lax.broadcasted_iota(jnp.int32, (groups, SUB, LANES), 1)
    step = 1
    while step < SUB:
        if backward:
            shift, ok = SUB - step, place < SUB - step
        else:
            shift, ok = step, place >= step
        a_far = jnp.where(ok, pltpu.roll(a, shift, 1), 1.0)
        b_far = jnp.where(ok, pltpu.roll(b, shift, 1), 0.0)
        b = a * b_far + b
        a = a * a_far
        step *= 2
    order = range(groups - 1, -1, -1) if backward else range(groups)
    edge = 0 if backward else SUB - 1
    a_in = jnp.ones((1, LANES), F32)
    b_in = jnp.zeros((1, LANES), F32)
    a_out, b_out = [None] * groups, [None] * groups
    for g in order:
        a_out[g] = a[g] * a_in
        b_out[g] = a[g] * b_in + b[g]
        a_in = a_out[g][edge : edge + 1]
        b_in = b_out[g][edge : edge + 1]
    return jnp.concatenate(a_out, 0), jnp.concatenate(b_out, 0), a_in, b_in


def head_kernel(order_ref):
    order_ref[...] = jnp.zeros_like(order_ref)


def pack_kernel(x_ref, cot_ref, doc_ref, bias_ref, rate_ref, order_ref, send_ref, own_ref):
    rows, width = x_ref.shape
    half = width // 2
    first = lax.axis_index("core") == 0
    for r, ref in enumerate((x_ref, cot_ref)):
        both = ref[...].astype(F32)
        send_ref[r * rows : (r + 1) * rows, :] = jnp.where(first, both[:, half:], both[:, :half])
        own_ref[r * rows : (r + 1) * rows, :] = jnp.where(first, both[:, :half], both[:, half:])
    doc = jnp.broadcast_to(doc_ref[...].astype(F32), (SUB, rows))
    doc = jnp.concatenate([doc] * (half // rows), axis=1)
    send_ref[2 * rows : 2 * rows + SUB, :] = doc
    own_ref[2 * rows : 2 * rows + SUB, :] = doc


def local_scans(pack_ref, w_ref, bias_ref, rate_ref, x_ref, k1_ref, k2_ref, k3_ref, k4_ref, cum_ref, ls_ref, pc_ref, la_ref):
    rows, half = x_ref.shape
    core = lax.axis_index("core")
    row = lax.broadcasted_iota(jnp.int32, (rows, LANES), 0)
    x_ref[...] = pack_ref[:rows].astype(BF16)
    rate8 = -8.0 * jnp.where(core == 0, rate_ref[:, :half], rate_ref[:, half:])
    pre = jnp.dot(x_ref[...], w_ref[core], preferred_element_type=F32) + bias_ref[pl.ds(core, 1), :]
    keep = 1.0 - jnp.transpose(jnp.broadcast_to(pack_ref[2 * rows : 2 * rows + 1, :rows], (LANES, rows)))
    kept = keep > 0.5
    ends = []
    for part in range(half // LANES):
        lanes = slice(part * LANES, (part + 1) * LANES)
        rgate = jax.nn.sigmoid(pre[:, lanes])
        igate = jax.nn.sigmoid(pre[:, half + part * LANES : half + (part + 1) * LANES])
        x = pack_ref[:rows, lanes]
        rate = rate8[:, lanes]
        decay = jnp.exp(rate * rgate)
        carry = decay * keep
        square = decay * decay
        root = jnp.sqrt(1.0 - square + 0.01)
        scale = jnp.where(kept, root, 1.0)
        dscale = jnp.where(kept, -square / root, 0.0)
        slope = rate * (rgate * (1.0 - rgate))
        k4 = scale * igate
        drive = k4 * x
        k1_ref[:, lanes] = carry * slope
        k2_ref[:, lanes] = igate * x * dscale * slope
        k3_ref[:, lanes] = drive * (1.0 - igate)
        k4_ref[:, lanes] = k4
        cum, state, product, last = column_scan(carry, drive, False)
        cum_ref[:, lanes] = cum
        ls_ref[:, lanes] = state
        ahead = jnp.where(row == rows - 1, 1.0, pltpu.roll(carry, rows - 1, 0))
        pc, adjoint, _, top = column_scan(ahead, pack_ref[rows : 2 * rows, lanes], True)
        pc_ref[:, lanes] = pc
        la_ref[:, lanes] = adjoint
        ends.append((product, last, carry[0:1] * top))
    return ends


def own_kernel(pack_ref, w_ref, bias_ref, rate_ref, summary_ref, *refs):
    for part, values in enumerate(local_scans(pack_ref, w_ref, bias_ref, rate_ref, *refs)):
        for i, value in enumerate(values):
            summary_ref[i, part : part + 1, :] = value


def got_kernel(pack_ref, w_ref, bias_ref, rate_ref, own_ref, summary_ref, *refs):
    core = lax.axis_index("core")
    ends = local_scans(pack_ref, w_ref, bias_ref, rate_ref, *refs)
    for part, values in enumerate(ends):
        for i, value in enumerate(values):
            summary_ref[i, pl.ds(core * len(ends) + part, 1), :] = own_ref[i, part : part + 1, :]
            summary_ref[i, pl.ds((1 - core) * len(ends) + part, 1), :] = value


def spread_kernel(summary_ref, _, spread_ref):
    summary = summary_ref[...]
    for j in range(spread_ref.shape[0]):
        spread_ref[j] = summary


def fold(all_ref, order, kind, base, wanted=None):
    product = jnp.ones(all_ref.shape[2:], F32)
    value = jnp.zeros(all_ref.shape[2:], F32)
    for z in order:
        a, b = all_ref[base + z, 0], all_ref[base + z, kind]
        if wanted is not None:
            a, b = jnp.where(wanted(z), a, 1.0), jnp.where(wanted(z), b, 0.0)
        value = a * value + b
        product = product * a
    return product, value


def edges(all_ref, kind, x, z, n_x, n_z, backward):
    half = all_ref.shape[2] // 2
    cores = (slice(0, half), slice(half, 2 * half))
    near, far = (cores[1], cores[0]) if backward else cores
    order = range(n_z - 1, -1, -1) if backward else range(n_z)
    apply = lambda link, at, value: link[0][at] * value + link[1][at]
    carried = jnp.zeros((half, LANES), F32)
    for i in range(n_x - 1, 0, -1) if backward else range(n_x - 1):
        link = fold(all_ref, order, kind, i * n_z)
        carried = jnp.where(i > x if backward else i < x, apply(link, far, apply(link, near, carried)), carried)
    base = x * n_z
    whole = fold(all_ref, order, kind, base)
    partial = fold(all_ref, order, kind, base, (lambda i: i > z) if backward else (lambda i: i < z))
    ahead = apply(partial, near, carried)
    behind = apply(partial, far, apply(whole, near, carried))
    return (behind, ahead) if backward else (ahead, behind)


def finish_kernel(n_x, n_z, all_ref, *refs):
    own, got, (out_ref, send_ref, dpre_ref, direct_ref, gw_ref) = refs[:9], refs[9:18], refs[18:]
    rows, half = out_ref.shape
    first = lax.axis_index("core") == 0
    at_x, at_z = lax.axis_index("x"), lax.axis_index("z")
    entering = edges(all_ref, 1, at_x, at_z, n_x, n_z, False)
    arriving = edges(all_ref, 2, at_x, at_z, n_x, n_z, True)
    row = lax.broadcasted_iota(jnp.int32, (rows, LANES), 0)
    weight_grad = 0.0
    for block, (x_ref, k1_ref, k2_ref, k3_ref, k4_ref, cum_ref, ls_ref, pc_ref, la_ref) in enumerate((own, got)):
        there = slice(block * rows, (block + 1) * rows)
        before = jnp.where(first, entering[block], entering[1 - block])
        after = jnp.where(first, arriving[block], arriving[1 - block])
        for part in range(half // LANES):
            lanes = slice(part * LANES, (part + 1) * LANES)
            start = before[part : part + 1]
            state = ls_ref[:, lanes] + cum_ref[:, lanes] * start
            if block == 0:
                out_ref[:, lanes] = state.astype(BF16)
            else:
                send_ref[:, lanes] = state
            previous = jnp.where(row == 0, start, pltpu.roll(state, 1, 0))
            adjoint = la_ref[:, lanes] + pc_ref[:, lanes] * after[part : part + 1]
            dpre_ref[there, lanes] = (adjoint * (k1_ref[:, lanes] * previous + k2_ref[:, lanes])).astype(BF16)
            far = slice(half + part * LANES, half + (part + 1) * LANES)
            dpre_ref[there, far] = (adjoint * k3_ref[:, lanes]).astype(BF16)
            direct_ref[there, lanes] = adjoint * k4_ref[:, lanes]
        weight_grad = weight_grad + lax.dot_general(
            x_ref[...], dpre_ref[there, :], (((0,), (0,)), ((), ())), preferred_element_type=F32
        )
    depth = SUB // 2
    low = lax.broadcasted_iota(jnp.int32, (SUB, 2 * half), 0) < depth
    for i in range(n_x):
        for pair in range(n_z // 2):
            u = weight_grad[i * 2 * n_z * depth + pair * SUB :][:SUB]
            v = weight_grad[(i * 2 + 1) * n_z * depth + pair * SUB :][:SUB]
            gw_ref[i * n_z + 2 * pair] = jnp.where(low, u, pltpu.roll(v, depth, 0))
            gw_ref[i * n_z + 2 * pair + 1] = jnp.where(low, pltpu.roll(u, depth, 0), v)


def inputs_kernel(dpre_ref, direct_ref, w_ref, states_ref, gx_ref, send_ref):
    rows = gx_ref.shape[0]
    core = lax.axis_index("core")
    back = lax.dot_general(dpre_ref[...], w_ref[core], (((1,), (1,)), ((), ())), preferred_element_type=F32)
    total = direct_ref[...] + back
    gx_ref[...] = total[:rows].astype(BF16)
    send_ref[:rows] = states_ref[...]
    send_ref[rows:] = total[rows:]


def unswap_kernel(out_ref, gx_ref, got_ref, outputs_ref, grad_ref, order_ref):
    rows, half = out_ref.shape
    first = lax.axis_index("core") == 0
    for r, (own, whole) in enumerate(((out_ref, outputs_ref), (gx_ref, grad_ref))):
        mine = own[...].astype(F32)
        got = got_ref[r * rows : (r + 1) * rows]
        whole[:, :half] = jnp.where(first, mine, got).astype(BF16)
        whole[:, half:] = jnp.where(first, got, mine).astype(BF16)
    order_ref[...] = jnp.zeros_like(order_ref)


def sum_kernel(pieces_ref, _, keep_ref, send_ref):
    total = pieces_ref[0]
    for j in range(1, pieces_ref.shape[0]):
        total = total + pieces_ref[j]
    first = lax.axis_index("core") == 0
    depth = SUB // 2
    keep_ref[...] = jnp.where(first, total[:depth], total[depth:])
    send_ref[...] = jnp.where(first, total[depth:], total[:depth])


def join_kernel(keep_ref, got_ref, grad_ref):
    first = lax.axis_index("core") == 0
    keep, got = keep_ref[...], got_ref[...]
    grad_ref[:, 0, :] = jnp.where(first, keep, got)
    grad_ref[:, 1, :] = jnp.where(first, got, keep)


def per_device(inputs, doc_start, gate_weight, gate_bias, decay_rate, cotangent):
    _, rows, width = inputs.shape
    head_dim, heads, wide = gate_weight.shape
    n_x, n_z = lax.axis_size("x"), lax.axis_size("z")
    chips = n_x * n_z
    half = width // 2
    depth = SUB // 2
    shape = jax.ShapeDtypeStruct
    vmem = pl.BlockSpec(memory_space=pltpu.VMEM)

    def call(kernel, operands, outs, name, scratch=(), cost=None):
        return pl.pallas_call(
            kernel,
            out_shape=outs,
            in_specs=[vmem] * len(operands),
            scratch_shapes=scratch,
            compiler_params=pltpu.CompilerParams(vmem_limit_bytes=16 << 20),
            cost_estimate=cost,
            name=name,
        )(*operands)

    swap = lambda value: lax.ppermute(value, "core", [(0, 1), (1, 0)])
    packed = shape((2 * rows + SUB, half), F32)
    gates = (jnp.moveaxis(gate_weight, 1, 0), gate_bias, decay_rate.reshape(1, width))
    cost = pl.CostEstimate(flops=4 * 10**9, bytes_accessed=4096, transcendentals=0)
    order = call(head_kernel, (), shape((SUB, LANES), F32), "head", cost=cost)
    operands = (inputs.reshape(rows, width), cotangent.reshape(rows, width), doc_start, *gates[1:], order)
    send, own = call(pack_kernel, operands, [packed] * 2, "pack")
    got = swap(send)
    fields = [shape((rows, half), BF16)] + [shape((rows, half), F32)] * 8
    tiles = half // LANES
    summary, *own = call(own_kernel, (own, *gates), [shape((3, tiles, LANES), F32)] + fields, "own_scans")
    summary, *got = call(got_kernel, (got, *gates, summary), [shape((3, 2 * tiles, LANES), F32)] + fields, "got_scans")
    met = lax.ppermute(order, "x", [(i, i ^ 1) for i in range(n_x)])
    spread = call(spread_kernel, (summary, met), shape((chips, 3, 2 * tiles, LANES), F32), "spread")
    everyone = lax.all_to_all(spread, ("x", "z"), 0, 0)
    out, states, dpre, direct, gw = call(
        lambda *refs: finish_kernel(n_x, n_z, *refs),
        (everyone, *own, *got),
        [
            shape((rows, half), BF16),
            shape((rows, half), F32),
            shape((2 * rows, wide), BF16),
            shape((2 * rows, half), F32),
            shape((chips, SUB, wide), F32),
        ],
        "finish",
    )
    pieces = lax.all_to_all(gw, ("x", "z"), 0, 0)
    gx, send = call(
        inputs_kernel, (dpre, direct, gates[0], states), [shape((rows, half), BF16), shape((2 * rows, half), F32)], "grad_inputs"
    )
    outputs, grad_inputs, order = call(
        unswap_kernel, (out, gx, swap(send)), [shape((rows, width), BF16)] * 2 + [shape((SUB, LANES), F32)], "unswap"
    )
    keep, give = call(sum_kernel, (pieces, order), [shape((depth, wide), F32)] * 2, "sum")
    grad_gate_weight = call(join_kernel, (keep, swap(give)), shape((depth, heads, wide), F32), "join")
    return (outputs[None], grad_inputs[None], grad_gate_weight)


def solution(mesh):
    n_dp, n_ctx, n_mp = mesh.devices.shape
    fine = Mesh(mesh.devices.reshape(n_dp // 2, 2, n_ctx, n_mp), ("x", "core", "z", "mp"))
    place = ("x", "core", "z")
    return jax.shard_map(
        per_device,
        mesh=fine,
        in_specs=(P(None, place, "mp"), P(None, place), P(None, "mp", None), P("mp", None), P("mp"), P(None, place, "mp")),
        out_specs=(P(None, place, "mp"), P(None, place, "mp"), P(place, "mp", None)),
        check_vma=False,
    )
```
